32 devices in a mesh: aux: 4 (over y, x), occ: 8 (over z, core).
Axes of the slice: x: 2, y: 2, z: 4, core: 2. Of those that a mesh axis runs over, the one named last changes fastest.
Arguments:
- factor: bfloat16 [6144, 8, 1536], P('aux', 'occ'), may hold values from -0.67578125 to 0.67578125
- occ_energy: float32 [1024], replicated, may hold values from -3 to -0.5
- vir_energy: float32 [3072], replicated, may hold values from 0.5 to 4
- occ_pick: int32 [8], replicated, may hold values from 0 to 1023
- vir_pick: int32 [1536], replicated, may hold values from 0 to 3071
Outputs:
- gamma: float32 [6144, 8, 1536], P('aux', 'occ')
The draws below stay inside these ranges and needn't reach their ends.
All inputs are finite; a program needn't handle non-finite values.
Results may differ from the reference program's by a relative error of at most 0.0024.
Values may be sent and summed in bfloat16 or wider, within the bound.
No kernel may reach another device: no remote copies, remote signals or barrier semaphores. Data moves between devices by JAX's collectives and lax.ppermute only.
A program may use at most 192 MiB of HBM per device.

```python
import jax
import jax.numpy as jnp
from jax import lax

NAUX = 6144
V = 1536
NOCC_ALL = 1024
NVIR_ALL = 3072
OCC_DEV = 1
OCC = 8
N_OCC = 8


def place_ends(entries, rng, low, top_value):
    shape = entries.shape
    spot = [jax.random.randint(jax.random.fold_in(rng, axis), (), 0, shape[axis]) for axis in range(len(shape))]
    entries = entries.at[tuple(spot)].set(low)
    longest = shape.index(max(shape))
    spot[longest] = (spot[longest] + 1) % shape[longest]
    return entries.at[tuple(spot)].set(top_value)


def shard_levels(stream_key, dims, pieces, least, top_value):
    def one(dim, shards_of):
        draws = jax.random.uniform(jax.random.fold_in(jax.random.fold_in(stream_key, 6), dim), (shards_of,), jnp.float32, least / len(pieces), top_value / len(pieces))
        return jnp.repeat(jnp.exp(draws), dims[dim] // shards_of).reshape((-1,) + (1,) * (len(dims) - dim - 1))

    factor_of = one(*pieces[0])
    for cut in pieces[1:]:
        factor_of = factor_of * one(*cut)
    return factor_of


def gaussian(stream_key, shape, scale, bound, pieces=(), held_as=jnp.bfloat16):
    drawn = scale * jax.random.normal(stream_key, shape, jnp.float32)
    if pieces:
        drawn = drawn * shard_levels(stream_key, shape, pieces, -0.22, 0.18)
    return jnp.clip(drawn, -bound, bound).astype(held_as)


def setup_inputs(seed: int = 0) -> dict:
    keys = jax.random.split(jax.random.key(seed), 6)
    return {
        "factor": gaussian(keys[0], (NAUX, OCC, V), (NAUX ** -0.25), 0.67578125, ((0, 4), (1, 8))),
        "occ_energy": jnp.clip(jax.random.uniform(keys[1], (NOCC_ALL,), jnp.float32, -3.0, -0.5), -3.0, -0.5),
        "vir_energy": jnp.clip(jax.random.uniform(keys[2], (NVIR_ALL,), jnp.float32, 0.5, 4.0), 0.5, 4.0),
        "occ_pick": place_ends(jax.random.randint(keys[3], (OCC,), 0, NOCC_ALL), jax.random.fold_in(keys[3], 1), 0, NOCC_ALL - 1).astype(jnp.int32),
        "vir_pick": place_ends(jax.random.randint(keys[4], (V,), 0, NVIR_ALL), jax.random.fold_in(keys[4], 1), 0, NVIR_ALL - 1).astype(jnp.int32),
    }


def reference(factor, occ_energy, vir_energy, occ_pick, vir_pick):
    occ_levels = occ_energy[occ_pick]
    vir_levels = vir_energy[vir_pick]

    def one_orbital(orbital):
        left_block = lax.dynamic_index_in_dim(factor, orbital, axis=1, keepdims=False)
        density = jnp.zeros((NAUX, V), jnp.float32)
        home = orbital // OCC_DEV
        for distance in (1, 2):
            for member in range(OCC_DEV):
                partner = (((home - distance) % N_OCC) * OCC_DEV + member).astype(jnp.int32)
                right_block = lax.dynamic_index_in_dim(factor, partner, axis=1, keepdims=False)
                integrals = lax.dot_general(left_block, right_block, (((0,), (0,)), ((), ())), preferred_element_type=jnp.float32)
                divisor = occ_levels[orbital] + occ_levels[partner] - vir_levels[:, None] - vir_levels[None, :]
                amplitudes = (integrals / divisor).astype(jnp.bfloat16)
                density = density + lax.dot_general(right_block, amplitudes, (((1,), (1,)), ((), ())), preferred_element_type=jnp.float32)
        return density

    stacked = lax.map(one_orbital, jnp.arange(OCC, dtype=jnp.int32))
    return jnp.transpose(stacked, (1, 0, 2))
```

```python
import jax
import jax.numpy as jnp
from jax import lax
from jax.experimental import pallas as pl
from jax.experimental.pallas import tpu as pltpu
from jax.sharding import PartitionSpec as P

LANES = 128
NEAR_SHARES = (2, 4, 6)
FAR_ORDER = (2, 1, 0)
GROUPS = ((0, 1), (2,), (3,), (4,), (5,))
TOP = 32768.0
VMEM_LIMIT = 24 << 20


def shifted(block, distance):
    size = lax.axis_size("occ")
    return lax.ppermute(block, "occ", [((i - distance) % size, i) for i in range(size)])


def swapped(block, bit):
    size = lax.axis_size("aux")
    return lax.ppermute(block, "aux", [(i, i ^ (1 << bit)) for i in range(size)])


def contract(left, right, dims):
    return lax.dot_general(left, right, (dims, ((), ())), preferred_element_type=jnp.float32)


def add_product(density, places, terms, linear):
    rows = terms[0][0].shape[0]
    part = terms[0][1][0].shape[0]
    count = len(terms[0][1])
    cols = part * count
    step = rows // 6 if rows % 96 == 0 else rows
    groups = cols // LANES

    def kernel(places_ref, *refs):
        refs = list(refs)
        density_ref = refs.pop(0) if density is not None else None
        term_refs = [(refs.pop(0), [refs.pop(0) for _ in range(count)]) for _ in terms]
        out_ref = refs.pop(0)
        full_ref = refs.pop(0) if linear else out_ref
        for q in range(count):
            spot = pl.ds(pl.multiple_of(places_ref[q], LANES), part)
            total = None
            for block_ref, piece_refs in term_refs:
                value = lax.dot_general(
                    block_ref[...], piece_refs[q][...], (((1,), (1,)), ((), ())), preferred_element_type=jnp.float32
                )
                total = value if total is None else total + value
            if density is not None:
                total = total + density_ref[:, spot]
            full_ref[:, spot] = total
        if linear:
            for g in range(groups):
                out_ref[pl.ds(g, step, stride=groups), :] = full_ref[:, g * LANES : (g + 1) * LANES]

    operands, in_specs = [], []
    if density is not None:
        operands.append(density)
        in_specs.append(pl.BlockSpec((step, cols), lambda r, _: (r, 0)))
    for block, pieces in terms:
        inner = block.shape[1]
        operands.append(block)
        in_specs.append(pl.BlockSpec((step, inner), lambda r, _: (r, 0)))
        for piece in pieces:
            operands.append(piece)
            in_specs.append(pl.BlockSpec((part, inner), lambda r, _: (0, 0)))
    if linear:
        out_shape = jax.ShapeDtypeStruct((rows * groups, LANES), jnp.float32)
        out_spec = pl.BlockSpec((step * groups, LANES), lambda r, _: (r, 0))
    else:
        out_shape = jax.ShapeDtypeStruct((rows, cols), jnp.float32)
        out_spec = pl.BlockSpec((step, cols), lambda r, _: (r, 0))
    return pl.pallas_call(
        kernel,
        grid_spec=pltpu.PrefetchScalarGridSpec(
            num_scalar_prefetch=1,
            grid=(rows // step,),
            in_specs=in_specs,
            out_specs=out_spec,
            scratch_shapes=[pltpu.VMEM((step, cols), jnp.float32)] if linear else [],
        ),
        out_shape=out_shape,
        compiler_params=pltpu.CompilerParams(vmem_limit_bytes=VMEM_LIMIT),
    )(places, *operands)


def on_device(factor, occ_energy, vir_energy, occ_pick, vir_pick):
    aux_count = lax.axis_size("aux")
    occ_count = lax.axis_size("occ")
    aux_place = lax.axis_index("aux")
    occ_place = lax.axis_index("occ")
    rows, _, virtuals = factor.shape
    bits = aux_count.bit_length() - 1
    own = factor[:, 0, :]

    unit = virtuals // sum(NEAR_SHARES)
    widths = [unit * s for s in NEAR_SHARES]
    starts = [sum(widths[:c]) for c in range(len(widths))]

    near = []
    source = own
    for c, (s, w) in enumerate(zip(starts, widths)):
        piece = lax.slice_in_dim(source, s, s + w, axis=1)
        if c == 0:
            source, piece = lax.optimization_barrier((source, piece))
        else:
            piece, _ = lax.optimization_barrier((piece, near[-1]))
        near.append(shifted(piece, 1))
    work = [(1, c, near[c]) for c in range(len(near))]
    work += [(2, c, shifted(near[c], 1)) for c in FAR_ORDER]


    half = virtuals // 2
    part = half // 2
    first_bits = (0, bits - 1)
    mine = [(aux_place >> b) & 1 for b in first_bits]
    keep_start = [h * half + mine[h] * part for h in range(2)]
    send_start = [h * half + (1 - mine[h]) * part for h in range(2)]
    places = jnp.stack([keep_start[0], send_start[0], keep_start[1], send_start[1]]).astype(jnp.int32)
    keep_left = [lax.dynamic_slice_in_dim(own, s, part, 1) for s in keep_start]
    send_left = [lax.dynamic_slice_in_dim(own, s, part, 1) for s in send_start]
    keep_left, send_left = lax.optimization_barrier((keep_left, send_left))
    first = [contract(send_left[h], near[0], ((0,), (0,))) for h in range(2)]
    occ_levels = jnp.take(occ_energy, occ_pick)
    vir_levels = jnp.take(vir_energy, vir_pick)
    keep_levels = [lax.dynamic_slice_in_dim(vir_levels, s, part) for s in keep_start]
    own_level = lax.dynamic_index_in_dim(occ_levels, occ_place, keepdims=False)

    top = jnp.max(jnp.abs(source)).astype(jnp.float32)
    top = jnp.full((8, LANES), top, jnp.float32)
    tops = jnp.stack([top, shifted(top, 1), shifted(top, 2)])
    for b in range(bits):
        tops = jnp.maximum(tops, swapped(tops, b))
    roots = jnp.minimum((TOP / (rows * aux_count)) ** 0.5 / jnp.maximum(tops[:, 0, 0], 1e-37), 1e18)
    scales = [roots[0] * roots[1], roots[0] * roots[2]]

    terms = []
    for k, (distance, c, block) in enumerate(work):
        other_level = lax.dynamic_index_in_dim(occ_levels, (occ_place - distance) % occ_count, keepdims=False)
        col_levels = lax.slice_in_dim(vir_levels, starts[c], starts[c] + widths[c])
        scale = scales[distance - 1]
        unscale = 1.0 / scale
        pieces = []
        for h in range(2):
            if k == 0:
                leaving = first[h]
            else:
                leaving = (contract(send_left[h], block, ((0,), (0,))) * scale).astype(jnp.float16)
            total = lax.optimization_barrier(contract(keep_left[h], block, ((0,), (0,))))
            row_levels, cols = keep_levels[h], col_levels
            route = [first_bits[h]] + [b for b in range(bits) if b != first_bits[h]]
            for stage, b in enumerate(route):
                if stage:
                    leaving = (total * scale).astype(jnp.float16) if k else total
                came = swapped(leaving, b)
                if stage == bits - 1:
                    came, row_levels, cols = lax.optimization_barrier((came, row_levels, cols))
                total = total + (came.astype(jnp.float32) * unscale if k else came)
            divisor = own_level + other_level - row_levels[:, None] - cols[None, :]
            kept = (total / divisor).astype(jnp.bfloat16)
            pieces += [kept, swapped(kept, first_bits[h])]
        terms.append((block, pieces))

    density = None
    for g, members in enumerate(GROUPS):
        last = g == len(GROUPS) - 1
        density = add_product(density, places, [terms[m] for m in members], last)
    return density.reshape(rows, 1, virtuals)


def solution(mesh):
    placed = (P("aux", "occ", None), P(), P(), P(), P())

    return jax.shard_map(
        on_device, mesh=mesh, in_specs=placed, out_specs=P("aux", "occ", None), check_vma=False
    )
```

```python
import jax
import jax.numpy as jnp
from jax import lax
from jax.experimental import pallas as pl
from jax.experimental.pallas import tpu as pltpu
from jax.sharding import PartitionSpec as P

LANES = 128
NEAR_SHARES = (2, 4, 6)
FAR_ORDER = (2, 1, 0)
GROUPS = ((0, 1), (2,), (3,), (4,), (5,))
TOP = 32768.0
VMEM_LIMIT = 24 << 20


def shifted(block, distance):
    size = lax.axis_size("occ")
    return lax.ppermute(block, "occ", [((i - distance) % size, i) for i in range(size)])


def swapped(block, bit):
    size = lax.axis_size("aux")
    return lax.ppermute(block, "aux", [(i, i ^ (1 << bit)) for i in range(size)])


def picked(values, picks):
    spots = lax.broadcasted_iota(jnp.int32, (values.shape[0], picks.shape[0]), 0)
    return jnp.sum(jnp.where(spots == picks[None, :], values[:, None], 0.0), axis=0)


def contract(left, right, dims):
    return lax.dot_general(left, right, (dims, ((), ())), preferred_element_type=jnp.float32)


def add_product(density, places, terms, linear):
    rows = terms[0][0].shape[0]
    part = terms[0][1][0].shape[0]
    count = len(terms[0][1])
    cols = part * count
    step = rows // 6 if rows % 96 == 0 else rows
    groups = cols // LANES

    def kernel(places_ref, *refs):
        refs = list(refs)
        density_ref = refs.pop(0) if density is not None else None
        term_refs = [(refs.pop(0), [refs.pop(0) for _ in range(count)]) for _ in terms]
        out_ref = refs.pop(0)
        full_ref = refs.pop(0) if linear else out_ref
        for q in range(count):
            spot = pl.ds(pl.multiple_of(places_ref[q], LANES), part)
            total = None
            for block_ref, piece_refs in term_refs:
                value = lax.dot_general(
                    block_ref[...], piece_refs[q][...], (((1,), (1,)), ((), ())), preferred_element_type=jnp.float32
                )
                total = value if total is None else total + value
            if density is not None:
                total = total + density_ref[:, spot]
            full_ref[:, spot] = total
        if linear:
            for g in range(groups):
                out_ref[pl.ds(g, step, stride=groups), :] = full_ref[:, g * LANES : (g + 1) * LANES]

    operands, in_specs = [], []
    if density is not None:
        operands.append(density)
        in_specs.append(pl.BlockSpec((step, cols), lambda r, _: (r, 0)))
    for block, pieces in terms:
        inner = block.shape[1]
        operands.append(block)
        in_specs.append(pl.BlockSpec((step, inner), lambda r, _: (r, 0)))
        for piece in pieces:
            operands.append(piece)
            in_specs.append(pl.BlockSpec((part, inner), lambda r, _: (0, 0)))
    if linear:
        out_shape = jax.ShapeDtypeStruct((rows * groups, LANES), jnp.float32)
        out_spec = pl.BlockSpec((step * groups, LANES), lambda r, _: (r, 0))
    else:
        out_shape = jax.ShapeDtypeStruct((rows, cols), jnp.float32)
        out_spec = pl.BlockSpec((step, cols), lambda r, _: (r, 0))
    return pl.pallas_call(
        kernel,
        grid_spec=pltpu.PrefetchScalarGridSpec(
            num_scalar_prefetch=1,
            grid=(rows // step,),
            in_specs=in_specs,
            out_specs=out_spec,
            scratch_shapes=[pltpu.VMEM((step, cols), jnp.float32)] if linear else [],
        ),
        out_shape=out_shape,
        compiler_params=pltpu.CompilerParams(vmem_limit_bytes=VMEM_LIMIT),
    )(places, *operands)


def on_device(factor, occ_energy, vir_energy, occ_pick, vir_pick):
    aux_count = lax.axis_size("aux")
    occ_count = lax.axis_size("occ")
    aux_place = lax.axis_index("aux")
    occ_place = lax.axis_index("occ")
    rows, _, virtuals = factor.shape
    bits = aux_count.bit_length() - 1
    own = factor[:, 0, :]

    unit = virtuals // sum(NEAR_SHARES)
    widths = [unit * s for s in NEAR_SHARES]
    starts = [sum(widths[:c]) for c in range(len(widths))]

    near = []
    source = own
    room = (TOP / (rows * aux_count)) ** 0.5
    for c, (s, w) in enumerate(zip(starts, widths)):
        piece = lax.slice_in_dim(source, s, s + w, axis=1)
        if c == 0:
            source, piece = lax.optimization_barrier((source, piece))
        near.append(shifted(piece, 1))

    work = [(1, c, near[c]) for c in range(len(near))]
    work += [(2, c, shifted(near[c], 1)) for c in FAR_ORDER]


    half = virtuals // 2
    part = half // 2
    first_bits = (0, bits - 1)
    mine = [(aux_place >> b) & 1 for b in first_bits]
    keep_start = [h * half + mine[h] * part for h in range(2)]
    send_start = [h * half + (1 - mine[h]) * part for h in range(2)]
    places = jnp.stack([keep_start[0], send_start[0], keep_start[1], send_start[1]]).astype(jnp.int32)
    keep_left = [lax.dynamic_slice_in_dim(own, s, part, 1) for s in keep_start]
    send_left = [lax.dynamic_slice_in_dim(own, s, part, 1) for s in send_start]
    keep_left, send_left = lax.optimization_barrier((keep_left, send_left))
    top = jnp.full((8, LANES), jnp.max(jnp.abs(source)), jnp.float32)
    for b in range(bits):
        top = jnp.maximum(top, swapped(top, b))
    root = jnp.minimum(room / jnp.maximum(top, 1e-37), 1e18)
    partner_roots = [shifted(root, d) for d in (1, 2)]
    scales = [(root * other)[0, 0] for other in partner_roots]

    first = [contract(send_left[h], near[0], ((0,), (0,))) for h in range(2)]
    occ_levels = picked(occ_energy, occ_pick)
    vir_levels = picked(vir_energy, vir_pick)
    keep_levels = [lax.dynamic_slice_in_dim(vir_levels, s, part) for s in keep_start]
    own_level = lax.dynamic_index_in_dim(occ_levels, occ_place, keepdims=False)

    terms = []
    for k, (distance, c, block) in enumerate(work):
        other_level = lax.dynamic_index_in_dim(occ_levels, (occ_place - distance) % occ_count, keepdims=False)
        col_levels = lax.slice_in_dim(vir_levels, starts[c], starts[c] + widths[c])
        scale = scales[distance - 1]
        unscale = 1.0 / scale
        pieces = []
        for h in range(2):
            if k == 0:
                leaving = first[h]
            else:
                leaving = (contract(send_left[h], block, ((0,), (0,))) * scale).astype(jnp.float16)
            total = lax.optimization_barrier(contract(keep_left[h], block, ((0,), (0,))))
            row_levels, cols = keep_levels[h], col_levels
            route = [first_bits[h]] + [b for b in range(bits) if b != first_bits[h]]
            for stage, b in enumerate(route):
                if stage:
                    leaving = (total * scale).astype(jnp.float16) if k else total
                came = swapped(leaving, b)
                if stage == bits - 1:
                    came, row_levels, cols = lax.optimization_barrier((came, row_levels, cols))
                total = total + (came.astype(jnp.float32) * unscale if k else came)
            divisor = own_level + other_level - row_levels[:, None] - cols[None, :]
            kept = (total / divisor).astype(jnp.bfloat16)
            pieces += [kept, swapped(kept, first_bits[h])]
        terms.append((block, pieces))

    density = None
    for g, members in enumerate(GROUPS):
        last = g == len(GROUPS) - 1
        density = add_product(density, places, [terms[m] for m in members], last)
    return density.reshape(rows, 1, virtuals)


def solution(mesh):
    placed = (P("aux", "occ", None), P(), P(), P(), P())

    return jax.shard_map(on_device, mesh=mesh, in_specs=placed, out_specs=P("aux", "occ", None), check_vma=False)
```
